32 devices in a mesh: groups: 2 (over y), ulysses: 8 (over z, x), seq: 2 (over core).
Axes of the slice: x: 2, y: 2, z: 4, core: 2. Of those that a mesh axis runs over, the one named last changes fastest.
Arguments:
- query_states: bfloat16 [2048, 8192], P(('groups', 'ulysses', 'seq')), parts along dimension 0, may hold values from -6 to 6
- key_states: bfloat16 [2048, 1024], P(('groups', 'ulysses', 'seq')), parts along dimension 0, may hold values from -6 to 6
- value_states: bfloat16 [2048, 1024], P(('groups', 'ulysses', 'seq')), parts along dimension 0, may hold values from -6 to 6
- turn_ids: int32 [2048], P('groups'), parts along dimension 0, may hold values from 0 to 3, never falling along the last dimension, each value on 1 to 512 neighbouring positions
- judge_positions: int32 [256], P('groups'), parts along dimension 0, may hold values from 0 to 1023, as said below
Outputs:
- attended_states: bfloat16 [2048, 8192], P(('groups', 'ulysses', 'seq')), parts along dimension 0
The draws below stay inside these ranges and needn't reach their ends.
There are 2 independent parts, one for each index of `groups`. The reference program is written for one: setup_inputs(seed, part) draws one part's arguments, and reference() takes and returns one part's arrays. A program takes and returns all parts, laid end to end along the dimension named above; each array names one. Nothing has to cross between parts.
Inputs may be any that keep to these rules, and one draw needn't show every extreme that they name: `turn_ids`: turn numbers never fall along the conversation; every turn spans 1 to 512 tokens, one exactly that many. `judge_positions`: distinct positions, 0 and 1023 among them.
All inputs are finite; a program needn't handle non-finite values.
Results may differ from the reference program's by a relative error of at most 0.004.
Values may be sent and summed in bfloat16 or wider, within the bound.
No kernel may reach another device: no remote copies, remote signals or barrier semaphores. Data moves between devices by JAX's collectives and lax.ppermute only.
A program may use at most 64 MiB of HBM per device.

```python
import math
import jax
import jax.numpy as jnp
import numpy as np
from jax import lax

QUERY_HEADS = 64
KEY_HEADS = 8
HEAD_DIM = 128
TURN_COUNT = 4
TOTAL_TOKENS = 1024
JUDGE_COUNT = 128


def draw_query_states(key, part):
    drawn = jnp.clip(jax.random.normal(jax.random.fold_in(key, 21), (TOTAL_TOKENS, QUERY_HEADS * HEAD_DIM), jnp.float32), -6.0, 6.0)
    return drawn.astype(jnp.bfloat16)


def draw_key_states(key, part):
    drawn = jnp.clip(jax.random.normal(jax.random.fold_in(key, 22), (TOTAL_TOKENS, KEY_HEADS * HEAD_DIM), jnp.float32), -6.0, 6.0)
    return drawn.astype(jnp.bfloat16)


def draw_judge_positions(key, part):
    inner = jax.random.permutation(jax.random.fold_in(key, 11), TOTAL_TOKENS - 2)[:JUDGE_COUNT - 2] + 1
    ends = jnp.array([0, TOTAL_TOKENS - 1], dtype=jnp.int32)
    return jnp.concatenate([ends, inner.astype(jnp.int32)])


def steps_of(stream_key, shape, shards, low, high):
    loudness, own = 1.0, jax.random.fold_in(stream_key, 6)
    for position, blocks in shards:
        heights = jnp.exp(jax.random.uniform(jax.random.fold_in(own, position), (blocks,), jnp.float32, low / len(shards), high / len(shards)))
        loudness = loudness * jnp.repeat(heights, shape[position] // blocks).reshape([-1 if axis == position else 1 for axis in range(len(shape))])
    return loudness


def split_up(amount, total, limit, slope):
    weights = [(1 << 20) // math.isqrt(grade ** slope) + 1 for grade in range(2, amount + 1)]
    spare, counts = total - limit - (amount - 1), [1] * (amount - 1)
    while spare > 0:
        movable = [i for i in range(amount - 1) if counts[i] < limit]
        pool, budget = sum([weights[i] for i in movable]), spare
        for i in movable:
            addition = min(limit - counts[i], max(1, budget * weights[i] // pool), spare)
            counts[i] = counts[i] + addition
            spare = spare - addition
    return np.array([limit] + counts)


def uneven_parts(key, count, total, limit, skew):
    if count == 2:
        one = jax.random.randint(key, (), max(1, total - limit), min(limit, total - 1) + 1)
        return jnp.stack([one, total - one])
    sizes = jnp.asarray(split_up(count, total, limit, skew), jnp.int32)
    pairs = (count - 1) // 2
    donor, taker = sizes[1:1 + 2 * pairs:2], sizes[2:2 + 2 * pairs:2]
    slack = jnp.minimum(donor - 1, limit - taker)
    moved = jax.random.randint(jax.random.fold_in(key, 1), (pairs,), 0, 1 << 20) % (slack + 1)
    sizes = sizes.at[1:1 + 2 * pairs:2].set(donor - moved).at[2:2 + 2 * pairs:2].set(taker + moved)
    return sizes[jax.random.permutation(jax.random.fold_in(key, 2), count)]


def noise(own_key, dims, spread, limit, shards=(), kind=jnp.bfloat16):
    loudness = steps_of(own_key, dims, shards, -0.22, 0.18) if shards else 1.0
    values = jax.random.normal(own_key, dims, jnp.float32) * spread * loudness
    return jnp.minimum(jnp.maximum(values, -limit), limit).astype(kind)


def setup_inputs(seed: int = 0, part: int = 0) -> dict:
    key_of = jax.random.split(jax.random.key(seed), 6)
    own_keys = jax.random.split(jax.random.fold_in(key_of[5], part), 6)
    query_states = draw_query_states(jax.random.fold_in(jax.random.fold_in(key_of[5], part), 71), part)
    key_states = draw_key_states(jax.random.fold_in(jax.random.fold_in(key_of[5], part), 71), part)
    value_states = noise(own_keys[2], (TOTAL_TOKENS, KEY_HEADS * HEAD_DIM), 1.0, 6.0, ((0, 16),))
    turn_ids = jnp.searchsorted(jnp.cumsum(uneven_parts(own_keys[3], TURN_COUNT, TOTAL_TOKENS, TOTAL_TOKENS // 2, 1)), jnp.arange(TOTAL_TOKENS), side="right").astype(jnp.int32)
    judge_positions = draw_judge_positions(jax.random.fold_in(jax.random.fold_in(key_of[5], part), 71), part)
    return {"query_states": query_states, "key_states": key_states, "value_states": value_states, "turn_ids": turn_ids, "judge_positions": judge_positions}


floor_score = -1e+30

def reference(query_states, key_states, value_states, turn_ids, judge_positions):
    seq_total = TOTAL_TOKENS
    sharing = QUERY_HEADS // KEY_HEADS
    scaling = 1.0 / math.sqrt(HEAD_DIM)
    positions = jnp.arange(seq_total, dtype=jnp.int32)
    judged = jnp.any(positions[:, None] == judge_positions[None, :], axis=1)
    query_rows = query_states.reshape(seq_total, QUERY_HEADS, HEAD_DIM).transpose(1, 0, 2)
    key_rows = key_states.reshape(seq_total, KEY_HEADS, HEAD_DIM).transpose(1, 0, 2)
    value_rows = value_states.reshape(seq_total, KEY_HEADS, HEAD_DIM).transpose(1, 0, 2)
    step_rows = math.gcd(seq_total, 512)
    blocks = seq_total // step_rows

    def one_head(head_index):
        query_head = query_rows[head_index]
        key_head = key_rows[head_index // sharing]
        value_head = value_rows[head_index // sharing]

        def one_block(block_index):
            offset = (block_index * step_rows).astype(jnp.int32)
            query_block = lax.dynamic_slice_in_dim(query_head, offset, step_rows, 0)
            query_place = offset + jnp.arange(step_rows, dtype=jnp.int32)
            query_turn = lax.dynamic_slice_in_dim(turn_ids, offset, step_rows, 0)
            scores = jnp.dot(query_block, key_head.T, preferred_element_type=jnp.float32) * scaling
            visible = (positions[None, :] <= query_place[:, None]) & ((turn_ids[None, :] == query_turn[:, None]) | judged[None, :])
            scores = jnp.where(visible, scores, floor_score)
            peak = lax.optimization_barrier(jnp.max(scores, axis=1, keepdims=True))
            weights = jnp.exp(scores - peak)
            totals = lax.optimization_barrier(jnp.sum(weights, axis=1, keepdims=True))
            mixed = jnp.dot(weights.astype(jnp.bfloat16), value_head, preferred_element_type=jnp.float32) / totals
            return mixed.astype(jnp.bfloat16)
        return lax.map(one_block, jnp.arange(blocks, dtype=jnp.int32)).reshape(seq_total, HEAD_DIM)
    heads_out = lax.map(one_head, jnp.arange(QUERY_HEADS, dtype=jnp.int32))
    return heads_out.transpose(1, 0, 2).reshape(seq_total, QUERY_HEADS * HEAD_DIM)
```

```python
import functools
import math

import jax
import jax.numpy as jnp
from jax import lax
from jax.experimental import pallas as pl
from jax.experimental.pallas import tpu as pltpu
from jax.sharding import PartitionSpec as P

HEAD_DIM = 128
LANES = 128
hidden = -1e30
exponent_scale = math.log2(math.e) / math.sqrt(HEAD_DIM)


def attend_kernel(pieces, first, last, places, queries, *refs):
    keys = refs[:pieces]
    values = refs[pieces : 2 * pieces]
    refs = refs[2 * pieces :]
    bias_ref, refs = refs[0], refs[1:]
    if not first:
        (old_mixed, old_total, old_peak), refs = refs[:3], refs[3:]
    if last:
        out_ref, refs = refs[0], refs[1:]
    else:
        (new_mixed, new_total, new_peak), refs = refs[:3], refs[3:]
    score_ref, peak_ref = refs
    tokens = queries.shape[0]
    key_heads = keys[0].shape[1] // HEAD_DIM
    sharing = queries.shape[1] // (HEAD_DIM * key_heads)
    rows = sharing * tokens
    key_count = sum(ref.shape[0] for ref in keys)
    one_hot = jnp.where(
        lax.broadcasted_iota(jnp.int32, (rows, LANES), 0) % tokens
        == lax.broadcasted_iota(jnp.int32, (rows, LANES), 1),
        1.0,
        0.0,
    ).astype(jnp.bfloat16)
    bias = jnp.concatenate(
        [
            bias_ref[pl.ds(pl.multiple_of(places[p], tokens), keys[p].shape[0]), :]
            for p in range(pieces)
        ],
        0,
    )
    ones = jnp.ones((key_count, LANES), jnp.bfloat16)

    def score(head, slot):
        span = slice(head * HEAD_DIM, (head + 1) * HEAD_DIM)
        block = jnp.concatenate([ref[:, span] for ref in keys], 0)
        block = jnp.concatenate([block, bias], 1)
        stacked = jnp.concatenate(
            [
                queries[:, (head * sharing + a) * HEAD_DIM : (head * sharing + a + 1) * HEAD_DIM]
                for a in range(sharing)
            ],
            0,
        )
        stacked = jnp.concatenate([stacked, one_hot], 1)
        scores = lax.dot_general(
            stacked, block, (((1,), (1,)), ((), ())), preferred_element_type=jnp.float32
        )
        score_ref[slot] = scores
        peak_ref[slot] = jnp.broadcast_to(jnp.max(scores, axis=1, keepdims=True), (rows, LANES))

    def finish(head, slot):
        span = slice(head * HEAD_DIM, (head + 1) * HEAD_DIM)
        block = jnp.concatenate([ref[:, span] for ref in values], 0)
        block = jnp.concatenate([block, ones], 1)
        here = slice(head * rows, (head + 1) * rows)
        peak = peak_ref[slot]
        if not first:
            peak = jnp.maximum(peak, old_peak[here])
        weights = jnp.exp2((score_ref[slot] - peak[:, :1]) * exponent_scale)
        mixed = jnp.dot(
            weights.astype(jnp.bfloat16), block, preferred_element_type=jnp.float32
        )
        mixed, total = mixed[:, :HEAD_DIM], mixed[:, HEAD_DIM:]
        if not first:
            factor = jnp.exp2((old_peak[here] - peak) * exponent_scale)
            mixed = mixed + old_mixed[here] * factor
            total = total + old_total[here] * factor
        if last:
            result = (mixed / total).astype(jnp.bfloat16)
            for a in range(sharing):
                at = (head * sharing + a) * HEAD_DIM
                out_ref[:, at : at + HEAD_DIM] = result[a * tokens : (a + 1) * tokens]
        else:
            new_mixed[here] = mixed
            new_total[here] = total
            new_peak[here] = peak

    score(0, 0)
    for head in range(key_heads):
        if head + 1 < key_heads:
            score(head + 1, (head + 1) % 2)
        finish(head, head % 2)


def attend(queries, keys, values, places, bias, carried, last):
    pieces = len(keys)
    tokens = queries.shape[0]
    key_heads = keys[0].shape[1] // HEAD_DIM
    heads = queries.shape[1] // HEAD_DIM
    rows = heads // key_heads * tokens
    key_count = sum(k.shape[0] for k in keys)
    whole = pl.BlockSpec(memory_space=pltpu.VMEM)
    carry = jax.ShapeDtypeStruct((heads * tokens, LANES), jnp.float32)
    previous = () if carried is None else carried
    return pl.pallas_call(
        functools.partial(attend_kernel, pieces, carried is None, last),
        out_shape=jax.ShapeDtypeStruct(queries.shape, queries.dtype) if last else (carry,) * 3,
        in_specs=[pl.BlockSpec(memory_space=pltpu.SMEM)]
        + [whole] * (2 + 2 * pieces + len(previous)),
        out_specs=whole if last else (whole,) * 3,
        scratch_shapes=[
            pltpu.VMEM((2, rows, key_count), jnp.float32),
            pltpu.VMEM((2, rows, LANES), jnp.float32),
        ],
        cost_estimate=pl.CostEstimate(
            flops=4 * 2 * heads * tokens * key_count * HEAD_DIM,
            transcendentals=heads * tokens * key_count,
            bytes_accessed=2 * (queries.size * 2 + 2 * pieces * keys[0].size),
        ),
        compiler_params=pltpu.CompilerParams(vmem_limit_bytes=24 * 1024 * 1024),
        name="attend",
    )(jnp.stack(places).astype(jnp.int32), queries, *keys, *values, bias, *previous)


def mask_bias(turn_ids, judge_positions, start, tokens):
    total = turn_ids.shape[0]
    key_place = jnp.arange(total + tokens, dtype=jnp.int32)
    key_turn = jnp.pad(turn_ids, (0, tokens))
    judged = jnp.any(key_place[:, None] == judge_positions[None, :], axis=1)
    query_place = start + jnp.arange(LANES, dtype=jnp.int32)
    query_turn = jnp.pad(lax.dynamic_slice_in_dim(turn_ids, start, tokens, 0), (0, LANES - tokens))
    visible = (key_place[:, None] <= query_place[None, :]) & (
        (key_turn[:, None] == query_turn[None, :]) | judged[:, None]
    )
    return jnp.where(visible, 0.0, hidden).astype(jnp.bfloat16)


def ring(queries, keys, values, bias, tokens):
    axes = ("ulysses", "seq")
    count = lax.axis_size("ulysses") * lax.axis_size("seq")
    here = lax.axis_index(axes)
    step = [(d, (d + 1) % count) for d in range(count)]
    carried = attend(queries, [keys], [values], [here * tokens], bias, None, False)

    def body(i, state):
        k, v, carried = state
        k = lax.ppermute(k, axes, step)
        v = lax.ppermute(v, axes, step)
        source = lax.rem(here - i + count, count)
        return k, v, attend(queries, [k], [v], [source * tokens], bias, carried, False)

    keys, values, carried = lax.fori_loop(1, count - 1, body, (keys, values, carried))
    keys = lax.ppermute(keys, axes, step)
    values = lax.ppermute(values, axes, step)
    source = lax.rem(here + 1, count)
    return attend(queries, [keys], [values], [source * tokens], bias, carried, True)


def shards(query_states, key_states, value_states, turn_ids, judge_positions):
    tokens = query_states.shape[0]
    ulysses_count = lax.axis_size("ulysses")
    stripe_count = lax.axis_size("seq")
    member = lax.axis_index("ulysses")
    stripe = lax.axis_index("seq")
    total = turn_ids.shape[0]
    bias = mask_bias(turn_ids, judge_positions, (member * stripe_count + stripe) * tokens, tokens)
    if ulysses_count > 8 or ulysses_count % 2 or stripe_count != 2:
        return ring(query_states, key_states, value_states, bias, tokens)

    def place(owner, core):
        return jnp.where(owner >= 0, (owner * stripe_count + core) * tokens, total)

    def over(array, shift):
        return lax.ppermute(
            array, "ulysses", [(u, u + shift) for u in range(ulysses_count - shift)]
        )

    def pair(array):
        return lax.ppermute(array, "ulysses", [(u, u ^ 1) for u in range(ulysses_count)])

    def core(array):
        return lax.ppermute(array, "seq", [(0, 1), (1, 0)])

    groups = []
    for layer in range(ulysses_count // 2):
        near = [a if layer == 0 else over(a, 2 * layer) for a in (key_states, value_states)]
        far = [pair(a) for a in near]
        pieces = [near, far, [core(a) for a in near], [core(a) for a in far]]
        owners = [member - 2 * layer, (member ^ 1) - 2 * layer]
        places = [place(o, c) for c in (stripe, 1 - stripe) for o in owners]
        groups.append(([p[0] for p in pieces], [p[1] for p in pieces], places))

    carried = None
    calls = [groups[:2], groups[2:]] if len(groups) > 2 else [groups]
    for index, call in enumerate(calls):
        carried = attend(
            query_states,
            sum([g[0] for g in call], []),
            sum([g[1] for g in call], []),
            sum([g[2] for g in call], []),
            bias,
            carried,
            index == len(calls) - 1,
        )
    return carried


def solution(mesh):
    placed = (
        P(("groups", "ulysses", "seq"), None),
        P(("groups", "ulysses", "seq"), None),
        P(("groups", "ulysses", "seq"), None),
        P("groups"),
        P("groups"),
    )
    return jax.shard_map(
        shards,
        mesh=mesh,
        in_specs=placed,
        out_specs=P(("groups", "ulysses", "seq"), None),
        check_vma=False,
    )
```

```python
import functools
import math

import jax
import jax.numpy as jnp
from jax import lax
from jax.experimental import pallas as pl
from jax.experimental.pallas import tpu as pltpu
from jax.sharding import PartitionSpec as P


HEAD_DIM = 128
LANES = 128
hidden = -1e30
exponent_scale = math.log2(math.e) / math.sqrt(HEAD_DIM)

WHOLE = pl.BlockSpec(memory_space=pltpu.VMEM)
SCALARS = pl.BlockSpec(memory_space=pltpu.SMEM)


def device_start(tokens):
    return lax.axis_index(("ulysses", "seq")) * tokens


def prepare_kernel(tokens, queries, keys, values, turn_ids, judge_positions, *refs):
    bias, staged, (turns, judges), sems = refs[0], refs[1:4], refs[4:6], refs[6]
    copies = [
        pltpu.make_async_copy(src, dst, sems.at[i])
        for i, (src, dst) in enumerate(
            zip((turn_ids, judge_positions, queries, keys, values), (turns, judges, *staged))
        )
    ]
    for copy in copies:
        copy.start()
    block = device_start(tokens) // LANES
    rows = lax.broadcasted_iota(jnp.int32, (LANES, LANES), 0)
    lanes = lax.broadcasted_iota(jnp.int32, (LANES, LANES), 1)
    query_place = block * LANES + lanes
    copies[0].wait()
    copies[1].wait()
    query_turn = turns[pl.ds(block, 1), :]

    def chunk(r, carry):
        key_place = r * LANES + rows
        spread = jnp.broadcast_to(turns[pl.ds(r, 1), :], (LANES, LANES))
        key_turn = jnp.sum(jnp.where(rows == lanes, spread, 0), axis=1, keepdims=True)
        hits = jnp.zeros((LANES, LANES), jnp.int32)
        for row in range(judges.shape[0]):
            hits = hits + jnp.where(key_place == judges[row : row + 1, :], 1, 0)
        judged = jnp.max(hits, axis=1, keepdims=True) > 0
        visible = (key_place <= query_place) & ((key_turn == query_turn) | judged)
        bias[pl.ds(pl.multiple_of(r * LANES, LANES), LANES), :] = jnp.where(
            visible, 0.0, hidden
        ).astype(jnp.bfloat16)
        return carry

    lax.fori_loop(0, turns.shape[0], chunk, 0)
    for copy in copies[2:]:
        copy.wait()


def prepare(queries, keys, values, turn_ids, judge_positions):
    tokens = queries.shape[0]
    total = turn_ids.shape[0]
    turns, judges = turn_ids.reshape(-1, LANES), judge_positions.reshape(-1, LANES)
    staged = [jax.ShapeDtypeStruct(a.shape, a.dtype) for a in (queries, keys, values)]
    return pl.pallas_call(
        functools.partial(prepare_kernel, tokens),
        out_shape=[jax.ShapeDtypeStruct((total, LANES), jnp.bfloat16), *staged],
        in_specs=[pl.BlockSpec(memory_space=pltpu.HBM)] * 5,
        out_specs=[WHOLE] * 4,
        scratch_shapes=[
            pltpu.VMEM(turns.shape, jnp.int32),
            pltpu.VMEM(judges.shape, jnp.int32),
            pltpu.SemaphoreType.DMA((5,)),
        ],
        cost_estimate=pl.CostEstimate(
            flops=total * LANES, transcendentals=0, bytes_accessed=2 * queries.size * 2
        ),
        compiler_params=pltpu.CompilerParams(vmem_limit_bytes=8 * 1024 * 1024),
        name="prepare",
    )(queries, keys, values, turns, judges)


def attend_kernel(locate, pieces, first, last, scalars, queries, *refs):
    keys, values, refs = refs[:pieces], refs[pieces : 2 * pieces], refs[2 * pieces :]
    bias_ref, refs = refs[0], refs[1:]
    if not first:
        (old_mixed, old_total, old_peak), refs = refs[:3], refs[3:]
    if last:
        out_ref, score_ref, peak_ref, result_ref, sems = refs
    else:
        new_mixed, new_total, new_peak, score_ref, peak_ref = refs
    tokens = queries.shape[0]
    key_heads = keys[0].shape[1] // HEAD_DIM
    sharing = queries.shape[1] // (HEAD_DIM * key_heads)
    rows = sharing * tokens
    key_count = sum(ref.shape[0] for ref in keys)
    offset = device_start(tokens) % LANES
    one_hot = jnp.where(
        lax.broadcasted_iota(jnp.int32, (rows, LANES), 0) % tokens + offset
        == lax.broadcasted_iota(jnp.int32, (rows, LANES), 1),
        1.0,
        0.0,
    ).astype(jnp.bfloat16)
    places = locate(scalars)
    bias = jnp.concatenate(
        [
            bias_ref[pl.ds(pl.multiple_of(place * tokens, tokens), ref.shape[0]), :]
            for place, ref in zip(places, keys)
        ],
        0,
    )
    ones = jnp.ones((key_count, LANES), jnp.bfloat16)
    spans = [(at, min(LANES, key_count - at)) for at in range(0, key_count, LANES)]

    def part(array, span):
        start, width = span
        return array[:, start : start + width] if array.shape[1] == key_count else array[:, :width]

    def score(head, slot):
        span = slice(head * HEAD_DIM, (head + 1) * HEAD_DIM)
        block = jnp.concatenate([ref[:, span] for ref in keys], 0)
        block = jnp.concatenate([block, bias], 1)
        stacked = jnp.concatenate(
            [
                queries[:, (head * sharing + a) * HEAD_DIM : (head * sharing + a + 1) * HEAD_DIM]
                for a in range(sharing)
            ],
            0,
        )
        stacked = jnp.concatenate([stacked, one_hot], 1)
        scores = lax.dot_general(
            stacked, block, (((1,), (1,)), ((), ())), preferred_element_type=jnp.float32
        )
        score_ref[slot] = scores
        peak = functools.reduce(jnp.maximum, (part(scores, at) for at in spans))
        peak_ref[slot] = jnp.broadcast_to(jnp.max(peak, axis=1, keepdims=True), (rows, LANES))

    def written(head):
        span = slice(head * sharing * HEAD_DIM, (head + 1) * sharing * HEAD_DIM)
        return pltpu.make_async_copy(result_ref.at[:, span], out_ref.at[:, span], sems.at[head])

    def finish(head, slot):
        span = slice(head * HEAD_DIM, (head + 1) * HEAD_DIM)
        block = jnp.concatenate([ref[:, span] for ref in values], 0)
        block = jnp.concatenate([block, ones], 1)
        here = slice(head * rows, (head + 1) * rows)
        peak = peak_ref[slot]
        if not first:
            peak = jnp.maximum(peak, old_peak[here])
        scores = score_ref[slot]
        weights = jnp.concatenate(
            [
                jnp.exp2((part(scores, at) - part(peak, at)) * exponent_scale).astype(jnp.bfloat16)
                for at in spans
            ],
            1,
        )
        mixed = jnp.dot(weights, block, preferred_element_type=jnp.float32)
        mixed, total = mixed[:, :HEAD_DIM], mixed[:, HEAD_DIM:]
        if not first:
            factor = jnp.exp2((old_peak[here] - peak) * exponent_scale)
            mixed = mixed + old_mixed[here] * factor
            total = total + old_total[here] * factor
        if last:
            result = (mixed / total).astype(jnp.bfloat16)
            for a in range(sharing):
                at = (head * sharing + a) * HEAD_DIM
                result_ref[:, at : at + HEAD_DIM] = result[a * tokens : (a + 1) * tokens]
            written(head).start()
        else:
            new_mixed[here] = mixed
            new_total[here] = total
            new_peak[here] = peak

    score(0, 0)
    for head in range(key_heads):
        if head + 1 < key_heads:
            score(head + 1, (head + 1) % 2)
        finish(head, head % 2)
    if last:
        for head in range(key_heads):
            written(head).wait()


def attend(queries, keys, values, bias, locate, scalars, carried, last):
    pieces = len(keys)
    tokens = queries.shape[0]
    columns = keys[0].shape[1]
    heads = queries.shape[1] // HEAD_DIM
    rows = heads // (columns // HEAD_DIM) * tokens
    key_count = sum(k.shape[0] for k in keys)
    carry = jax.ShapeDtypeStruct((heads * tokens, LANES), jnp.float32)
    previous = () if carried is None else carried
    return pl.pallas_call(
        functools.partial(attend_kernel, locate, pieces, carried is None, last),
        out_shape=jax.ShapeDtypeStruct(queries.shape, queries.dtype) if last else (carry,) * 3,
        in_specs=[SCALARS] + [WHOLE] * (2 + 2 * pieces + len(previous)),
        out_specs=pl.BlockSpec(memory_space=pl.ANY) if last else (WHOLE,) * 3,
        scratch_shapes=[
            pltpu.VMEM((2, rows, key_count), jnp.float32),
            pltpu.VMEM((2, rows, LANES), jnp.float32),
        ]
        + (
            [
                pltpu.VMEM(queries.shape, queries.dtype),
                pltpu.SemaphoreType.DMA((columns // HEAD_DIM,)),
            ]
            if last
            else []
        ),
        cost_estimate=pl.CostEstimate(
            flops=4 * 2 * heads * tokens * key_count * HEAD_DIM,
            transcendentals=heads * tokens * key_count,
            bytes_accessed=2 * queries.size * 2 + 4 * key_count * columns,
        ),
        compiler_params=pltpu.CompilerParams(vmem_limit_bytes=16 * 1024 * 1024),
        name="attend",
    )(scalars, queries, *keys, *values, bias, *previous)


def ring(queries, keys, values, bias):
    axes = ("ulysses", "seq")
    count = lax.axis_size("ulysses") * lax.axis_size("seq")
    step = [(d, (d + 1) % count) for d in range(count)]

    def locate(scalars):
        return [lax.rem(lax.axis_index(axes) - scalars[0] + count, count)]

    def absorb(k, v, i, carried, last):
        scalars = jnp.full((1,), i, jnp.int32)
        return attend(queries, [k], [v], bias, locate, scalars, carried, last)

    def body(i, state):
        k, v, carried = state
        k, v = lax.ppermute(k, axes, step), lax.ppermute(v, axes, step)
        return k, v, absorb(k, v, i, carried, False)

    state = (keys, values, absorb(keys, values, 0, None, False))
    keys, values, carried = lax.fori_loop(1, count - 1, body, state)
    keys, values = lax.ppermute(keys, axes, step), lax.ppermute(values, axes, step)
    return absorb(keys, values, count - 1, carried, True)


def paired(ulysses_count, stripe_count):
    return ulysses_count == 2 * 4 and stripe_count == 2


def shards(query_states, key_states, value_states, turn_ids, judge_positions):
    ulysses_count = lax.axis_size("ulysses")
    stripe_count = lax.axis_size("seq")
    bias, *staged = prepare(
        query_states, key_states, value_states, turn_ids, judge_positions
    )
    if not paired(ulysses_count, stripe_count):
        return ring(staged[0], key_states, value_states, bias)

    def flip(bits, array):
        return lax.ppermute(array, "ulysses", [(u, u ^ bits) for u in range(ulysses_count)])

    def core(array):
        return lax.ppermute(array, "seq", [(0, 1), (1, 0)])

    def named(function, arrays):
        out = []
        for array in arrays:
            out.append(function(array))
        return out

    def family(near, bits, held=None):
        far = named(functools.partial(flip, 1), near)
        near_core = named(core, near)
        far_core = named(core, far)
        return [
            (near if held is None else held, bits, 0),
            (far, bits ^ 1, 0),
            (near_core, bits, 1),
            (far_core, bits ^ 1, 1),
        ]

    def call(members, carried, last):
        def locate(scalars):
            member, stripe = lax.axis_index("ulysses"), lax.axis_index("seq")
            return [
                (member ^ bits) * stripe_count + (stripe ^ other) for _, bits, other in members
            ]

        keys, values = [m[0][0] for m in members], [m[0][1] for m in members]
        return attend(
            staged[0], keys, values, bias, locate, jnp.zeros((1,), jnp.int32), carried, last
        )

    own = [key_states, value_states]
    o = family(own, 0, staged[1:])
    a = family(named(functools.partial(flip, 2), own), 2)
    c = family(named(functools.partial(flip, 4), own), 4)
    b = family(named(functools.partial(flip, 6), own), 6)
    carried = call([*o, *a], None, False)
    carried = call(c, carried, False)
    return call(b, carried, True)


def solution(mesh):
    placed = (
        P(("groups", "ulysses", "seq"), None),
        P(("groups", "ulysses", "seq"), None),
        P(("groups", "ulysses", "seq"), None),
        P("groups"),
        P("groups"),
    )

    return jax.shard_map(
        shards,
        mesh=mesh,
        in_specs=placed,
        out_specs=P(("groups", "ulysses", "seq"), None),
        check_vma=False,
    )
```
